128 devices in a mesh: row: 16 (over z, x_lo, core), col: 8 (over y, x_hi).
Axes of the slice: x: 4 (x_hi: 2, x_lo: 2; x = x_hi * 2 + x_lo), y: 4, z: 4, core: 2. Of those that a mesh axis runs over, the one named last changes fastest.
Arguments:
- covariance: float32 [16384, 16384], P('row', 'col'), may hold values from -3 to 5, as said below
- obs_cells: int32 [2, 16384], P(None, ('row', 'col')), may hold values from 0 to 255
- pred_cells: int32 [2, 512], replicated, may hold values from 0 to 255
- targets: float32 [16384, 256], P(('row', 'col')), may hold values from -1.5 to 1.5
- cross_sum: float32 [16384, 512], P(('row', 'col')), may hold values from -1.8 to 1.8
- prior_mean: float32 [512, 256], replicated, may hold values from -6 to 6
Outputs:
- factor_state: float32 [16384, 16384], P('row', 'col')
- reduced_targets: float32 [16384, 256], P(('row', 'col'))
- cross_next: float32 [16384, 512], P(('row', 'col'))
- predicted: float32 [512, 256], replicated
The draws below stay inside these ranges and needn't reach their ends.
Inputs may be any that keep to these rules, and one draw needn't show every extreme that they name: covariance is symmetric and positive definite.
All inputs are finite; a program needn't handle non-finite values.
Results may differ from the reference program's by a relative error of at most 0.00007.
Values sent between devices are 32-bit elements; how exact they have to be, the bound alone decides.
No kernel may reach another device: no remote copies, remote signals or barrier semaphores. Data moves between devices by JAX's collectives and lax.ppermute only.
A program may use at most 128 MiB of HBM per device.

```python
import math
import jax
import jax.numpy as jnp
from jax import lax

TILE = 1024
RHS_COLS = 256
POINTS = 512
GRID = 256
RANGE = 16
ORDER = 16384


def draw_covariance(key, part):
    key_g = jax.random.fold_in(key, 11)
    key_d = jax.random.fold_in(key, 12)
    limit = math.sqrt(3.0)
    factors = jax.random.uniform(key_g, (ORDER, TILE), jnp.float32, -limit, limit)
    diagonal = jnp.exp(jax.random.uniform(key_d, (ORDER,), jnp.float32, math.log(0.5), math.log(2.0)))
    product = jnp.dot(factors, factors.T, precision=jax.lax.Precision.HIGHEST) / TILE
    product = 0.5 * (product + product.T)
    places = jnp.arange(ORDER)
    return product.at[places, places].add(diagonal)


def place_ends(values, key, low, largest):
    index_at = [jax.random.randint(jax.random.fold_in(key, axis), (), 0, length) for axis, length in enumerate(values.shape)]
    main_axis = values.shape.index(max(values.shape))
    neighbour = index_at[:main_axis] + [(index_at[main_axis] + 1) % values.shape[main_axis]] + index_at[main_axis + 1:]
    return values.at[tuple(index_at)].set(low).at[tuple(neighbour)].set(largest)


def shard_levels(own_key, extent, split, low, high):
    gain, own = 1.0, jax.random.fold_in(own_key, 6)
    for dim, shards_of in split:
        steps = jnp.exp(jax.random.uniform(jax.random.fold_in(own, dim), (shards_of,), jnp.float32, low / len(split), high / len(split)))
        gain = gain * jnp.repeat(steps, extent[dim] // shards_of).reshape([-1 if axis == dim else 1 for axis in range(len(extent))])
    return gain


def normal_values(rng, extent, deviation, most, shards=(), kind=jnp.bfloat16):
    array = deviation * jax.random.normal(rng, extent, jnp.float32)
    if shards:
        array = array * shard_levels(rng, extent, shards, -0.22, 0.18)
    return jnp.clip(array, -most, most).astype(kind)


def setup_inputs(seed: int = 0) -> dict:
    seeds = jax.random.split(jax.random.key(seed), 7)
    return {
        "covariance": draw_covariance(jax.random.fold_in(seeds[6], 71), 0),
        "obs_cells": place_ends(jax.random.randint(seeds[1], (2, ORDER), 0, GRID), jax.random.fold_in(seeds[1], 1), 0, GRID - 1).astype(jnp.int32),
        "pred_cells": place_ends(jax.random.randint(seeds[2], (2, POINTS), 0, GRID), jax.random.fold_in(seeds[2], 1), 0, GRID - 1).astype(jnp.int32),
        "targets": normal_values(seeds[3], (ORDER, RHS_COLS), 0.25, 1.5, ((0, 128),), jnp.float32),
        "cross_sum": normal_values(seeds[4], (ORDER, POINTS), 0.3, 1.8, ((0, 128),), jnp.float32),
        "prior_mean": normal_values(seeds[5], (POINTS, RHS_COLS), 1.0, 6.0, (), jnp.float32),
    }


root_three = math.sqrt(3.0)

def matern_tile(cells_a, cells_b):
    first = cells_a.astype(jnp.float32)
    second = cells_b.astype(jnp.float32)
    delta_x = first[0][:, None] - second[0][None, :]
    delta_y = first[1][:, None] - second[1][None, :]
    scaled = jnp.sqrt(delta_x * delta_x + delta_y * delta_y) * (root_three / RANGE)
    return (1.0 + scaled) * jnp.exp(-scaled)

def reference(covariance, obs_cells, pred_cells, targets, cross_sum, prior_mean):
    lead_factor = jnp.linalg.cholesky(covariance[:TILE, :TILE])
    panel = lax.linalg.triangular_solve(lead_factor, covariance[:, :TILE], left_side=False, lower=True, transpose_a=True)
    factor_state = covariance - jnp.dot(panel, panel.T, precision=lax.Precision.HIGHEST)
    factor_state = factor_state.at[:, :TILE].set(panel)
    factor_state = factor_state.at[:TILE, TILE:].set(jnp.zeros((TILE, ORDER - TILE), jnp.float32))
    kernel = matern_tile(obs_cells[:, :TILE], pred_cells)
    stacked = jnp.concatenate([targets[:TILE], kernel - cross_sum[:TILE]], axis=1)
    both = lax.linalg.triangular_solve(lead_factor, stacked, left_side=True, lower=True, transpose_a=False)
    solved = both[:, :RHS_COLS]
    lifted = both[:, RHS_COLS:]
    reduced_targets = targets - jnp.dot(panel, solved, precision=lax.Precision.HIGHEST)
    reduced_targets = reduced_targets.at[:TILE].set(solved)
    cross_next = cross_sum + jnp.dot(panel, lifted, precision=lax.Precision.HIGHEST)
    cross_next = cross_next.at[:TILE].set(lifted)
    predicted = prior_mean + jnp.dot(lifted.T, solved, precision=lax.Precision.HIGHEST)
    return (factor_state, reduced_targets, cross_next, predicted)
```

```python
import math

import jax
import jax.numpy as jnp
from jax import lax
from jax.experimental import pallas as pl
from jax.experimental.pallas import tpu as pltpu
from jax.sharding import PartitionSpec as P

RANGE = 16
BLOCK = 128
BAND = 32
GROUP = 8
STRIP = 256
AXES = ("row", "col")
HIGHEST = lax.Precision.HIGHEST
HIGH = lax.Precision.HIGH


root_three = math.sqrt(3.0)


def matern_tile(first, second):
    delta_x = first[0][:, None] - second[0][None, :]
    delta_y = first[1][:, None] - second[1][None, :]
    scaled = jnp.sqrt(delta_x * delta_x + delta_y * delta_y) * (root_three / RANGE)
    return (1.0 + scaled) * jnp.exp(-scaled)


def iota(shape, dim):
    return lax.broadcasted_iota(jnp.int32, shape, dim)


def dot(a, b):
    return jnp.dot(a, b, precision=HIGHEST, preferred_element_type=jnp.float32)


def dot_t(a, b):
    return lax.dot_general(
        a, b, (((0,), (0,)), ((), ())), precision=HIGHEST, preferred_element_type=jnp.float32
    )


def eliminate(rows, start):
    shape = (GROUP, BLOCK)
    lane, sub = iota(shape, 1), iota(shape, 0)
    count = len(rows)
    for g in range(count):
        base = start + GROUP * g
        cols = {
            (i, t): jnp.broadcast_to(rows[i][:, base + t : base + t + 1], shape)
            for i in range(g, count)
            for t in range(GROUP)
        }
        scale = jnp.ones(shape, jnp.float32)
        scaled = []
        for t in range(GROUP):
            j = base + t
            diag = cols[g, t]
            pivot = jnp.broadcast_to(diag[t : t + 1, :], shape)
            root = lax.rsqrt(pivot)
            root = root * (1.5 - 0.5 * pivot * root * root)
            inverse = root * root
            scale = jnp.where(sub == t, root, scale)
            own = jnp.where((lane == j) & (sub >= t), jnp.where(sub == t, 1.0, 0.0), rows[g])
            row = jnp.broadcast_to(own[t : t + 1, :], shape) * inverse
            below = jnp.where(sub > t, diag, 0.0)
            rows[g] = own - below * row
            scaled.append(jnp.where((lane > j) & (lane < base + GROUP), 0.0, row))
            for u in range(t + 1, GROUP):
                factor = jnp.broadcast_to(diag[u : u + 1, :], shape) * inverse
                for i in range(g, count):
                    cols[i, u] = cols[i, u] - (below if i == g else cols[i, t]) * factor
        for i in range(g + 1, count):
            rest = jnp.where((lane >= base) & (lane < base + GROUP), 0.0, rows[i])
            for t in range(GROUP):
                rest = rest - cols[i, t] * scaled[t]
            rows[i] = rest
        rows[g] = rows[g] * scale
    return rows


def invert_block(block):
    lane, sub = iota((BAND, BLOCK), 1), iota((BAND, BLOCK), 0)
    wide = iota((BLOCK, BLOCK), 1)
    done = []
    for start in range(0, BLOCK, BAND):
        rows = [block[start + g : start + g + GROUP, :] for g in range(0, BAND, GROUP)]
        band = jnp.concatenate(eliminate(rows, start), axis=0)
        upper = jnp.where(lane >= start + BAND, band, 0.0)
        clean = jnp.where((lane < start + BAND) & (lane > start + sub), 0.0, band)
        if start + BAND < BLOCK:
            block = jnp.where((wide >= start) & (wide < start + BAND), 0.0, block) - dot_t(upper, clean)
        done.append(jnp.where(lane > start + sub, 0.0, band))
    return jnp.concatenate(done, axis=0)


def strip_kernel(first, *refs):
    piece, above, out, work = refs[0], refs[1:-2], refs[-2], refs[-1]
    size = out.shape[1]
    if first:
        work[:, :first] = jnp.zeros((STRIP, first), jnp.float32)
    work[:, first:] = piece[...]
    for m, strip in enumerate(above):
        factor = strip[:, first : first + STRIP].T
        known = STRIP * (m + 1)
        work[:, :known] -= dot(factor, strip[:, :known])
        work[:, first:] -= dot(factor, strip[:, first:])
    lane = iota((BLOCK, size), 1)

    def step(s, _):
        here = pl.multiple_of(s * BLOCK, BLOCK)
        at = pl.multiple_of(first + s * BLOCK, BLOCK)
        inverse = invert_block(work[pl.ds(here, BLOCK), pl.ds(at, BLOCK)])
        work[pl.ds(here, BLOCK), :] = dot(inverse, work[pl.ds(here, BLOCK), :])
        work[pl.ds(here, BLOCK), pl.ds(at, BLOCK)] = inverse

        @pl.when(s == 0)
        def _():
            lower = work[BLOCK:, :]
            lower = jnp.where((lane >= first) & (lane < first + BLOCK), 0.0, lower)
            factor = work[:BLOCK, first + BLOCK : first + STRIP].T
            work[BLOCK:, :] = lower - dot(factor, work[:BLOCK, :])

        return 0

    lax.fori_loop(0, STRIP // BLOCK, step, 0)
    work[:BLOCK, first + BLOCK : first + STRIP] = jnp.zeros((BLOCK, BLOCK), jnp.float32)
    out[...] = work[...]


def factor_strip(piece, above):
    size = 1024
    first = STRIP * len(above)
    return pl.pallas_call(
        lambda *refs: strip_kernel(first, *refs),
        out_shape=jax.ShapeDtypeStruct((STRIP, size), jnp.float32),
        scratch_shapes=[pltpu.VMEM((STRIP, size), jnp.float32)],
        compiler_params=pltpu.CompilerParams(vmem_limit_bytes=40 << 20),
        name=f"factor_strip_{len(above)}",
    )(piece, *above)


def device(x, y, z, core):
    return (z * 4 + (x % 2) * 2 + core) * 8 + y * 2 + x // 2


def send(block, pairs):
    return lax.ppermute(block, AXES, pairs)


def pick(options, index):
    out = options[0]
    for k in range(1, len(options)):
        out = jnp.where(index == k, options[k], out)
    return out


ALL = [(x, y, z, k) for x in range(4) for y in range(4) for z in range(4) for k in range(2)]


def ring_gather(own, where, shift):
    half = own.shape[0] // 2
    left = send(own, shift(1))
    right = send(own, shift(-1))
    far_a = send(left[:half], shift(1))
    far_b = send(right[half:], shift(-1))
    rows = own.shape[0]
    out = jnp.zeros((4 * rows, own.shape[1]), own.dtype)
    out = lax.dynamic_update_slice(out, own, (rows * where, 0))
    out = lax.dynamic_update_slice(out, left, (rows * ((where + 3) % 4), 0))
    out = lax.dynamic_update_slice(out, right, (rows * ((where + 1) % 4), 0))
    far = rows * ((where + 2) % 4)
    out = lax.dynamic_update_slice(out, far_a, (far, 0))
    return lax.dynamic_update_slice(out, far_b, (far + half, 0))


def down_columns(tile, z, x_lo, core):
    rows = tile.shape[0] // 8
    mine = tile[:rows]
    for k in range(1, 8):
        h, q = k // 4, k % 4
        part = send(
            tile[rows * k : rows * (k + 1)],
            [(device(x, y, 0, 0), device(x, y, q, h)) for x in (0, 2) for y in range(4)],
        )
        mine = jnp.where((z == q) & (core == h), part, mine)
    crossed = send(
        mine,
        [(device(x, y, q, h), device(x + 1, y, q, h)) for x in (0, 2) for y in range(4) for q in range(4) for h in range(2)],
    )
    mine = jnp.where(x_lo == 0, mine, crossed)
    half = ring_gather(
        mine, z, lambda k: [(device(a, b, c, d), device(a, b, (c + k) % 4, d)) for a, b, c, d in ALL]
    )
    other = send(half, [(device(a, b, c, d), device(a, b, c, 1 - d)) for a, b, c, d in ALL])
    return jnp.concatenate([jnp.where(core == 0, half, other), jnp.where(core == 0, other, half)], axis=0)


def along_rows(tile, y, x_hi):
    rows = tile.shape[0] // 4
    mine = tile[:rows]
    for q in range(1, 4):
        part = send(
            tile[rows * q : rows * (q + 1)],
            [(device(x, 0, z, h), device(x, q, z, h)) for x in (0, 1) for z in range(4) for h in range(2)],
        )
        mine = jnp.where(y == q, part, mine)
    crossed = send(
        mine,
        [(device(x, q, z, h), device(x + 2, q, z, h)) for x in (0, 1) for q in range(4) for z in range(4) for h in range(2)],
    )
    mine = jnp.where(x_hi == 0, mine, crossed)
    return ring_gather(
        mine, y, lambda k: [(device(a, b, c, d), device(a, (b + k) % 4, c, d)) for a, b, c, d in ALL]
    )


def everywhere(piece, x, y, z, core):
    rows = piece.shape[0] // 4
    mine = piece[:rows]
    for q in range(1, 4):
        part = send(piece[rows * q : rows * (q + 1)], [(device(0, 0, 0, 0), device(0, q, 0, 0))])
        mine = jnp.where(y == q, part, mine)
    got = mine
    for k in (1, 3, 2):
        part = send(mine, [(device(0, b, 0, 0), device(k, b, 0, 0)) for b in range(4)])
        got = jnp.where(x == k, part, got)
    mine = got
    for k in (1, 3, 2):
        part = send(mine, [(device(a, b, 0, 0), device(a, b, k, 0)) for a in range(4) for b in range(4)])
        got = jnp.where(z == k, part, got)
    whole = ring_gather(
        got, y, lambda k: [(device(a, b, c, 0), device(a, (b + k) % 4, c, 0)) for a, b, c, d in ALL if d == 0]
    )
    other = send(whole, [(device(a, b, c, 0), device(a, b, c, 1)) for a, b, c, d in ALL if d == 0])
    return jnp.where(core == 0, whole, other)


def row_zero_gather(block, column):
    rows = block.shape[0]
    out = jnp.zeros((8 * rows, block.shape[1]), block.dtype)
    out = lax.dynamic_update_slice(out, block, (rows * column, 0))
    for k in range(1, 8):
        part = send(block, [(c, (c + k) % 8) for c in range(8)])
        out = lax.dynamic_update_slice(out, part, (rows * ((column - k) % 8), 0))
    return out


def body(covariance, obs_cells, pred_cells, targets, cross_sum, prior_mean):
    tile_size = covariance.shape[0]
    slab = targets.shape[0]
    width = targets.shape[1]
    row_index = lax.axis_index("row")
    column_index = lax.axis_index("col")
    z, x_lo, core = row_index // 4, (row_index // 2) % 2, row_index % 2
    y, x_hi = column_index // 2, column_index % 2
    x = 2 * x_hi + x_lo

    strips = []
    pieces = [
        everywhere(covariance[STRIP * k : STRIP * (k + 1), STRIP * k : tile_size], x, y, z, core)
        for k in range(tile_size // STRIP)
    ]
    mine = jnp.concatenate([targets, cross_sum], axis=1)
    cells = jnp.pad(obs_cells.astype(jnp.float32), ((0, 6), (0, 0)))
    top = row_zero_gather(mine, column_index)
    top_cells = row_zero_gather(cells, column_index)
    halves = [down_columns(covariance[:, k : k + tile_size], z, x_lo, core) for k in (0, tile_size)]
    top = down_columns(top, z, x_lo, core)
    top_cells = down_columns(top_cells, z, x_lo, core)
    row_tile = along_rows(covariance[:, :tile_size], y, x_hi)

    for piece in pieces:
        strips.append(factor_strip(piece, strips))
    packed = jnp.concatenate(strips, axis=0)
    keep = lax.broadcasted_iota(jnp.int32, packed.shape, 0) >= lax.broadcasted_iota(jnp.int32, packed.shape, 1)
    inverse = jnp.where(keep, packed, 0.0)

    lead_cells = top_cells.reshape(8, 8, slab)[:, :2].transpose(1, 0, 2).reshape(2, tile_size)
    kernel = matern_tile(lead_cells, pred_cells.astype(jnp.float32))
    stacked = jnp.concatenate([top[:, :width], kernel - top[:, width:]], axis=1)
    both = jnp.dot(inverse, stacked, precision=HIGH)
    panel_rows = lax.dot_general(row_tile, inverse, (((1,), (1,)), ((), ())), precision=HIGH)
    blocks = []
    for offset in range(2):
        panel = jnp.dot(inverse, halves[offset], precision=HIGH)
        local = covariance[:, offset * tile_size : (offset + 1) * tile_size]
        updated = local - jnp.dot(panel_rows, panel, precision=HIGH)
        updated = jnp.where(row_index == 0, jnp.zeros_like(updated), updated)
        if offset == 0:
            updated = jnp.where(column_index == 0, panel_rows, updated)
        blocks.append(updated)
    factor_state = jnp.concatenate(blocks, axis=1)
    solved = both[:, :width]
    lifted = both[:, width:]
    my_rows = lax.dynamic_slice_in_dim(panel_rows, column_index * slab, slab, 0)
    my_both = lax.dynamic_slice_in_dim(both, column_index * slab, slab, 0)
    change = jnp.dot(my_rows, both, precision=HIGH)
    reduced_targets = jnp.where(row_index == 0, my_both[:, :width], targets - change[:, :width])
    cross_next = jnp.where(row_index == 0, my_both[:, width:], cross_sum + change[:, width:])
    predicted = prior_mean + lax.dot_general(
        lifted, solved, (((0,), (0,)), ((), ())), precision=HIGH
    )
    return (factor_state, reduced_targets, cross_next, predicted)


def solution(mesh):
    in_specs = (
        P("row", "col"),
        P(None, AXES),
        P(),
        P(AXES, None),
        P(AXES, None),
        P(),
    )
    out_specs = (P("row", "col"), P(AXES, None), P(AXES, None), P())
    return jax.shard_map(body, mesh=mesh, in_specs=in_specs, out_specs=out_specs, check_vma=False)
```

```python
import math

import jax
import jax.numpy as jnp
from jax import lax
from jax.experimental import pallas as pl
from jax.experimental.pallas import tpu as pltpu
from jax.sharding import PartitionSpec as P

RANGE = 16
BLOCK = 128
BAND = 32
GROUP = 8
STRIP = 256
AXES = ("row", "col")
HIGHEST = lax.Precision.HIGHEST
HIGH = lax.Precision.HIGH


root_three = math.sqrt(3.0)


def matern_tile(first, second):
    delta_x = first[0][:, None] - second[0][None, :]
    delta_y = first[1][:, None] - second[1][None, :]
    scaled = jnp.sqrt(delta_x * delta_x + delta_y * delta_y) * (root_three / RANGE)
    return (1.0 + scaled) * jnp.exp(-scaled)


def iota(shape, dim):
    return lax.broadcasted_iota(jnp.int32, shape, dim)


def dot(a, b):
    return jnp.dot(a, b, precision=HIGHEST, preferred_element_type=jnp.float32)


def dot_t(a, b):
    return lax.dot_general(
        a, b, (((0,), (0,)), ((), ())), precision=HIGHEST, preferred_element_type=jnp.float32
    )


def eliminate(rows, start):
    shape = (GROUP, BLOCK)
    lane, sub = iota(shape, 1), iota(shape, 0)
    count = len(rows)
    for g in range(count):
        base = start + GROUP * g
        cols = {
            (i, t): jnp.broadcast_to(rows[i][:, base + t : base + t + 1], shape)
            for i in range(g, count)
            for t in range(GROUP)
        }
        scale = jnp.ones(shape, jnp.float32)
        scaled = []
        for t in range(GROUP):
            j = base + t
            diag = cols[g, t]
            pivot = jnp.broadcast_to(diag[t : t + 1, :], shape)
            root = lax.rsqrt(pivot)
            root = root * (1.5 - 0.5 * pivot * root * root)
            inverse = root * root
            scale = jnp.where(sub == t, root, scale)
            own = jnp.where((lane == j) & (sub >= t), jnp.where(sub == t, 1.0, 0.0), rows[g])
            row = jnp.broadcast_to(own[t : t + 1, :], shape) * inverse
            below = jnp.where(sub > t, diag, 0.0)
            rows[g] = own - below * row
            scaled.append(jnp.where((lane > j) & (lane < base + GROUP), 0.0, row))
            for u in range(t + 1, GROUP):
                factor = jnp.broadcast_to(diag[u : u + 1, :], shape) * inverse
                for i in range(g, count):
                    cols[i, u] = cols[i, u] - (below if i == g else cols[i, t]) * factor
        for i in range(g + 1, count):
            rest = jnp.where((lane >= base) & (lane < base + GROUP), 0.0, rows[i])
            for t in range(GROUP):
                rest = rest - cols[i, t] * scaled[t]
            rows[i] = rest
        rows[g] = rows[g] * scale
    return rows


def invert_block(block):
    lane, sub = iota((BAND, BLOCK), 1), iota((BAND, BLOCK), 0)
    wide = iota((BLOCK, BLOCK), 1)
    done = []
    for start in range(0, BLOCK, BAND):
        rows = [block[start + g : start + g + GROUP, :] for g in range(0, BAND, GROUP)]
        band = jnp.concatenate(eliminate(rows, start), axis=0)
        upper = jnp.where(lane >= start + BAND, band, 0.0)
        clean = jnp.where((lane < start + BAND) & (lane > start + sub), 0.0, band)
        if start + BAND < BLOCK:
            block = jnp.where((wide >= start) & (wide < start + BAND), 0.0, block) - dot_t(upper, clean)
        done.append(jnp.where(lane > start + sub, 0.0, band))
    return jnp.concatenate(done, axis=0)


def factor_kernel(flag, tile, out, work):
    size = tile.shape[0]
    count = size // BLOCK

    @pl.when(flag[0] == 1)
    def _():
        work[...] = tile[...]
        lane = iota((BLOCK, size), 1)

        def step(k, _):
            here = pl.multiple_of(k * BLOCK, BLOCK)
            inverse = invert_block(work[pl.ds(here, BLOCK), pl.ds(here, BLOCK)])
            work[pl.ds(here, BLOCK), :] = dot(inverse, work[pl.ds(here, BLOCK), :])
            work[pl.ds(here, BLOCK), pl.ds(here, BLOCK)] = inverse

            def update(i, _):
                at = pl.multiple_of(i * BLOCK, BLOCK)
                factor = work[pl.ds(here, BLOCK), pl.ds(at, BLOCK)].T
                rest = work[pl.ds(at, BLOCK), :]
                rest = jnp.where((lane >= here) & (lane < here + BLOCK), 0.0, rest)
                work[pl.ds(at, BLOCK), :] = rest - dot(factor, work[pl.ds(here, BLOCK), :])
                return 0

            lax.fori_loop(k + 1, count, update, 0)
            work[pl.ds(here, BLOCK), :] = jnp.where(lane > here + iota((BLOCK, size), 0), 0.0, work[pl.ds(here, BLOCK), :])
            return 0

        lax.fori_loop(0, count, step, 0)
        half = STRIP // 2
        out[:STRIP, :] = work[3 * STRIP :, :]
        out[STRIP : 2 * STRIP, : 3 * STRIP] = work[2 * STRIP : 3 * STRIP, : 3 * STRIP]
        out[STRIP : 2 * STRIP, 3 * STRIP :] = work[:STRIP, :STRIP]
        out[2 * STRIP :, : 2 * STRIP] = work[STRIP : STRIP + half, : 2 * STRIP]
        out[2 * STRIP :, 2 * STRIP :] = work[STRIP + half : 2 * STRIP, : 2 * STRIP]


def factor_tile(flag, tile):
    size = tile.shape[0]
    vmem = pl.BlockSpec(memory_space=pltpu.VMEM)
    return pl.pallas_call(
        factor_kernel,
        out_shape=jax.ShapeDtypeStruct((5 * STRIP // 2, size), jnp.float32),
        in_specs=[pl.BlockSpec(memory_space=pltpu.SMEM), vmem],
        out_specs=vmem,
        scratch_shapes=[pltpu.VMEM((size, size), jnp.float32)],
        compiler_params=pltpu.CompilerParams(vmem_limit_bytes=40 << 20),
        name="factor_tile",
    )(flag, tile)


def unpack(packed):
    low, middle, high = packed[:STRIP], packed[STRIP : 2 * STRIP], packed[2 * STRIP :]
    return jnp.concatenate(
        [
            jnp.pad(middle[:, 3 * STRIP :], ((0, 0), (0, 3 * STRIP))),
            jnp.pad(high[:, : 2 * STRIP], ((0, 0), (0, 2 * STRIP))),
            jnp.pad(high[:, 2 * STRIP :], ((0, 0), (0, 2 * STRIP))),
            jnp.pad(middle[:, : 3 * STRIP], ((0, 0), (0, STRIP))),
            low,
        ],
        axis=0,
    )


def device(x, y, z, core):
    return (z * 4 + (x % 2) * 2 + core) * 8 + y * 2 + x // 2


def send(block, pairs):
    return lax.ppermute(block, AXES, pairs)


def pick(options, index):
    out = options[0]
    for k in range(1, len(options)):
        out = jnp.where(index == k, options[k], out)
    return out


CHIPS = [(x, y, z) for x in range(4) for y in range(4) for z in range(4)]
ALL = [(x, y, z, k) for x, y, z in CHIPS for k in range(2)]


def tick(*groups):
    return lax.optimization_barrier(groups)


def ring_near(own, shift):
    return send(own, shift(1)), send(own, shift(-1))


def ring_far(near, shift):
    half = near[0].shape[0] // 2
    return send(near[0][:half], shift(1)), send(near[1][half:], shift(-1))


def ring_join(own, near, far, where):
    rows, half = own.shape[0], own.shape[0] // 2
    out = jnp.zeros((4 * rows, own.shape[1]), own.dtype)
    out = lax.dynamic_update_slice(out, own, (rows * where, 0))
    out = lax.dynamic_update_slice(out, near[0], (rows * ((where + 3) % 4), 0))
    out = lax.dynamic_update_slice(out, near[1], (rows * ((where + 1) % 4), 0))
    across = rows * ((where + 2) % 4)
    out = lax.dynamic_update_slice(out, far[0], (across, 0))
    return lax.dynamic_update_slice(out, far[1], (across + half, 0))


def z_ring(k):
    return [(device(a, b, c, 0), device(a, b, (c + k) % 4, 0)) for a, b, c in CHIPS]


def y_ring(k):
    return [(device(a, b, c, d), device(a, (b + k) % 4, c, d)) for a, b, c, d in ALL]


def y_ring_one(k):
    return [(device(a, b, c, 0), device(a, (b + k) % 4, c, 0)) for a, b, c in CHIPS]


def to_other_core(block, core):
    other = send(block, [(device(a, b, c, 0), device(a, b, c, 1)) for a, b, c in CHIPS])
    return jnp.where(core == 0, block, other)


def choose(own, parts, tests):
    for part, test in zip(parts, tests):
        own = jnp.where(test, part, own)
    return own


def ordered(own, other, first):
    return jnp.where(first, jnp.concatenate([own, other], axis=0), jnp.concatenate([other, own], axis=0))


def body(covariance, obs_cells, pred_cells, targets, cross_sum, prior_mean):
    tile_size = covariance.shape[0]
    slab = targets.shape[0]
    width = targets.shape[1]
    row_index = lax.axis_index("row")
    column_index = lax.axis_index("col")
    z, x_lo, core = row_index // 4, (row_index // 2) % 2, row_index % 2
    y, x_hi = column_index // 2, column_index % 2
    x = 2 * x_hi + x_lo

    mine = jnp.concatenate([targets, cross_sum], axis=1).reshape(tile_size, -1)
    cells = jnp.pad(obs_cells.astype(jnp.float32).reshape(8, -1), ((0, tile_size - 8), (0, 0)))
    extended = jnp.concatenate([covariance, mine, cells], axis=1)
    flag = ((row_index == 0) & (column_index == 0)).astype(jnp.int32).reshape(1)
    row_wide = covariance[:, :tile_size]
    quarter = tile_size // 4

    col_parts = [
        send(
            extended[quarter * q : quarter * (q + 1)],
            [(device(a, b, 0, 0), device(a, b, q, 0)) for a in (0, 2) for b in range(4)],
        )
        for q in range(1, 4)
    ]
    row_parts = [
        send(
            row_wide[quarter * q : quarter * (q + 1)],
            [(device(a, 0, c, d), device(a, q, c, d)) for a in (0, 1) for c in range(4) for d in range(2)],
        )
        for q in range(1, 4)
    ]
    packed = factor_tile(flag, row_wide)
    packed, col_parts, row_parts = tick(packed, col_parts, row_parts)
    col_own = choose(extended[:quarter], col_parts, [z == q for q in range(1, 4)])
    row_own = choose(row_wide[:quarter], row_parts, [y == q for q in range(1, 4)])

    rows = packed.shape[0] // 8
    parts = [send(packed[rows * c : rows * (c + 1)], [(0, c)]) for c in range(1, 8)]
    col_cross = send(
        col_own, [(device(a, b, c, 0), device(a + 1, b, c, 0)) for a in (0, 2) for b in range(4) for c in range(4)]
    )
    row_cross = send(
        row_own,
        [(device(a, b, c, d), device(a + 2, b, c, d)) for a in (0, 1) for b in range(4) for c in range(4) for d in range(2)],
    )
    eighth = choose(packed[:rows], parts, [column_index == c for c in range(1, 8)])
    parts = [
        send(eighth, [(device(a, b, 0, 0), device(a, b, k, 0)) for a in (0, 2) for b in range(4)]) for k in (1, 3, 2)
    ]
    eighth = choose(eighth, parts, [z == k for k in (1, 3, 2)])
    part = send(
        eighth, [(device(a, b, c, 0), device(a + 1, b, c, 0)) for a in (0, 2) for b in range(4) for c in range(4)]
    )
    eighth = jnp.where(x_lo == 0, eighth, part)
    eighth, col_cross, row_cross = tick(eighth, col_cross, row_cross)
    col_own = jnp.where(x_lo == 0, col_own, col_cross)
    row_own = jnp.where(x_hi == 0, row_own, row_cross)

    part = send(eighth, [(device(a, b, c, 0), device(a ^ 2, b, c, 0)) for a, b, c in CHIPS])
    col_near = ring_near(col_own, z_ring)
    row_near = ring_near(row_own, y_ring)
    pair = ordered(eighth, part, x_hi == 0)
    near = ring_near(pair, y_ring_one)
    near, col_near, row_near = tick(near, col_near, row_near)
    far = ring_far(near, y_ring_one)
    col_far = ring_far(col_near, z_ring)
    row_far = ring_far(row_near, y_ring)
    packed = to_other_core(ring_join(pair, near, far, y), core)
    row_tile = ring_join(row_own, row_near, row_far, y)
    column_tile = to_other_core(ring_join(col_own, col_near, col_far, z), core)
    inverse = unpack(packed)

    halves = [column_tile[:, :tile_size], column_tile[:, tile_size : 2 * tile_size]]
    shard = column_tile[:, 2 * tile_size :]
    part = send(shard, [(device(a, b, c, d), device(a ^ 2, b, c, d)) for a, b, c, d in ALL])
    shard = ordered(shard, part, x_hi == 0)
    near = ring_near(shard, y_ring)
    far = ring_far(near, y_ring)
    shards = ring_join(shard, near, far, y).reshape(8, tile_size, -1)
    top = shards[:, :, :96].reshape(tile_size, -1)
    lead_cells = shards[:, :8, 96:].reshape(8, 2, slab).transpose(1, 0, 2).reshape(2, tile_size)
    kernel = matern_tile(lead_cells, pred_cells.astype(jnp.float32))
    stacked = jnp.concatenate([top[:, :width], kernel - top[:, width:]], axis=1)
    both = jnp.dot(inverse, stacked, precision=HIGH)
    panel_rows = lax.dot_general(row_tile, inverse, (((1,), (1,)), ((), ())), precision=HIGH)
    blocks = []
    for offset in range(2):
        panel = jnp.dot(inverse, halves[offset], precision=HIGH)
        local = covariance[:, offset * tile_size : (offset + 1) * tile_size]
        updated = local - jnp.dot(panel_rows, panel, precision=HIGH)
        updated = jnp.where(row_index == 0, jnp.zeros_like(updated), updated)
        if offset == 0:
            updated = jnp.where(column_index == 0, panel_rows, updated)
        blocks.append(updated)
    factor_state = jnp.concatenate(blocks, axis=1)
    solved = both[:, :width]
    lifted = both[:, width:]
    my_rows = lax.dynamic_slice_in_dim(panel_rows, column_index * slab, slab, 0)
    my_both = lax.dynamic_slice_in_dim(both, column_index * slab, slab, 0)
    change = jnp.dot(my_rows, both, precision=HIGH)
    reduced_targets = jnp.where(row_index == 0, my_both[:, :width], targets - change[:, :width])
    cross_next = jnp.where(row_index == 0, my_both[:, width:], cross_sum + change[:, width:])
    predicted = prior_mean + lax.dot_general(
        lifted, solved, (((0,), (0,)), ((), ())), precision=HIGH
    )
    return (factor_state, reduced_targets, cross_next, predicted)


def solution(mesh):
    in_specs = (
        P("row", "col"),
        P(None, AXES),
        P(),
        P(AXES, None),
        P(AXES, None),
        P(),
    )
    out_specs = (P("row", "col"), P(AXES, None), P(AXES, None), P())
    return jax.shard_map(body, mesh=mesh, in_specs=in_specs, out_specs=out_specs, check_vma=False)
```

```python
import math

import jax
import jax.numpy as jnp
from jax import lax
from jax.experimental import pallas as pl
from jax.experimental.pallas import tpu as pltpu
from jax.sharding import PartitionSpec as P

RANGE = 16
BLOCK = 128
BAND = 32
GROUP = 8
STRIP = 256
AXES = ("row", "col")
HIGHEST = lax.Precision.HIGHEST
HIGH = lax.Precision.HIGH


root_three = math.sqrt(3.0)


def matern_tile(first, second):
    delta_x = first[0][:, None] - second[0][None, :]
    delta_y = first[1][:, None] - second[1][None, :]
    scaled = jnp.sqrt(delta_x * delta_x + delta_y * delta_y) * (root_three / RANGE)
    return (1.0 + scaled) * jnp.exp(-scaled)


def iota(shape, dim):
    return lax.broadcasted_iota(jnp.int32, shape, dim)


def dot(a, b):
    return jnp.dot(a, b, precision=HIGHEST, preferred_element_type=jnp.float32)


def dot_t(a, b):
    return lax.dot_general(
        a, b, (((0,), (0,)), ((), ())), precision=HIGHEST, preferred_element_type=jnp.float32
    )


def eliminate(rows, start):
    shape = (GROUP, BLOCK)
    lane, sub = iota(shape, 1), iota(shape, 0)
    count = len(rows)
    for g in range(count):
        base = start + GROUP * g
        cols = {
            (i, t): jnp.broadcast_to(rows[i][:, base + t : base + t + 1], shape)
            for i in range(g, count)
            for t in range(GROUP)
        }
        scale = jnp.ones(shape, jnp.float32)
        scaled = []
        for t in range(GROUP):
            j = base + t
            diag = cols[g, t]
            pivot = jnp.broadcast_to(diag[t : t + 1, :], shape)
            root = lax.rsqrt(pivot)
            root = root * (1.5 - 0.5 * pivot * root * root)
            inverse = root * root
            scale = jnp.where(sub == t, root, scale)
            own = jnp.where((lane == j) & (sub >= t), jnp.where(sub == t, 1.0, 0.0), rows[g])
            row = jnp.broadcast_to(own[t : t + 1, :], shape) * inverse
            below = jnp.where(sub > t, diag, 0.0)
            rows[g] = own - below * row
            scaled.append(jnp.where((lane > j) & (lane < base + GROUP), 0.0, row))
            for u in range(t + 1, GROUP):
                factor = jnp.broadcast_to(diag[u : u + 1, :], shape) * inverse
                for i in range(g, count):
                    cols[i, u] = cols[i, u] - (below if i == g else cols[i, t]) * factor
        for i in range(g + 1, count):
            rest = jnp.where((lane >= base) & (lane < base + GROUP), 0.0, rows[i])
            for t in range(GROUP):
                rest = rest - cols[i, t] * scaled[t]
            rows[i] = rest
        rows[g] = rows[g] * scale
    return rows


def invert_block(block):
    lane, sub = iota((BAND, BLOCK), 1), iota((BAND, BLOCK), 0)
    wide = iota((BLOCK, BLOCK), 1)
    done = []
    for start in range(0, BLOCK, BAND):
        rows = [block[start + g : start + g + GROUP, :] for g in range(0, BAND, GROUP)]
        band = jnp.concatenate(eliminate(rows, start), axis=0)
        upper = jnp.where(lane >= start + BAND, band, 0.0)
        clean = jnp.where((lane < start + BAND) & (lane > start + sub), 0.0, band)
        if start + BAND < BLOCK:
            block = jnp.where((wide >= start) & (wide < start + BAND), 0.0, block) - dot_t(upper, clean)
        done.append(jnp.where(lane > start + sub, 0.0, band))
    return jnp.concatenate(done, axis=0)


def half_kernel(last, packed, *refs):
    above, out, work = refs[:-2], refs[-2], refs[-1]
    half, size = work.shape
    first = half if last else 0
    if last:
        work[:, :half] = jnp.zeros((half, half), jnp.float32)
        work[:BLOCK, half:] = packed[2 * STRIP :, :half]
        work[BLOCK:STRIP, half:] = packed[2 * STRIP :, half:]
        work[STRIP:, half : half + STRIP] = jnp.zeros((STRIP, STRIP), jnp.float32)
        work[STRIP:, half + STRIP :] = packed[STRIP : 2 * STRIP, 3 * STRIP :]
        work[...] -= dot(above[0][:, half:].T, above[0][...])
    else:
        work[:STRIP, :] = packed[:STRIP, :]
        work[STRIP:, :STRIP] = jnp.zeros((STRIP, STRIP), jnp.float32)
        work[STRIP:, STRIP:] = packed[STRIP : 2 * STRIP, : 3 * STRIP]
    lane = iota((BLOCK, size), 1)
    count = half // BLOCK

    def step(k, _):
        here = pl.multiple_of(k * BLOCK, BLOCK)
        at = pl.multiple_of(first + k * BLOCK, BLOCK)
        inverse = invert_block(work[pl.ds(here, BLOCK), pl.ds(at, BLOCK)])
        work[pl.ds(here, BLOCK), :] = dot(inverse, work[pl.ds(here, BLOCK), :])
        work[pl.ds(here, BLOCK), pl.ds(at, BLOCK)] = inverse

        def update(i, _):
            row = pl.multiple_of(i * BLOCK, BLOCK)
            factor = work[pl.ds(here, BLOCK), pl.ds(pl.multiple_of(first + i * BLOCK, BLOCK), BLOCK)].T
            rest = work[pl.ds(row, BLOCK), :]
            rest = jnp.where((lane >= at) & (lane < at + BLOCK), 0.0, rest)
            work[pl.ds(row, BLOCK), :] = rest - dot(factor, work[pl.ds(here, BLOCK), :])
            return 0

        lax.fori_loop(k + 1, count, update, 0)
        clean = (lane > at + iota((BLOCK, size), 0)) & (lane < first + half)
        work[pl.ds(here, BLOCK), :] = jnp.where(clean, 0.0, work[pl.ds(here, BLOCK), :])
        return 0

    lax.fori_loop(0, count, step, 0)
    if last:
        out[:half, :half] = above[0][:, :half]
        out[:half, half:] = jnp.zeros((half, half), jnp.float32)
        out[half:, :] = work[...]
    else:
        out[...] = work[...]


def factor_half(packed, *above):
    size = packed.shape[1]
    last = bool(above)
    return pl.pallas_call(
        lambda *refs: half_kernel(last, *refs),
        out_shape=jax.ShapeDtypeStruct((size if last else size // 2, size), jnp.float32),
        scratch_shapes=[pltpu.VMEM((size // 2, size), jnp.float32)],
        compiler_params=pltpu.CompilerParams(vmem_limit_bytes=40 << 20),
        name="factor_low" if last else "factor_top",
    )(packed, *above)


def device(x, y, z, core):
    return (z * 4 + (x % 2) * 2 + core) * 8 + y * 2 + x // 2


def send(block, pairs):
    return lax.ppermute(block, AXES, pairs)


def pick(options, index):
    out = options[0]
    for k in range(1, len(options)):
        out = jnp.where(index == k, options[k], out)
    return out


CHIPS = [(x, y, z) for x in range(4) for y in range(4) for z in range(4)]
ALL = [(x, y, z, k) for x, y, z in CHIPS for k in range(2)]


def tick(*groups):
    return lax.optimization_barrier(groups)


def ring_near(own, shift):
    return send(own, shift(1)), send(own, shift(-1))


def ring_far(near, shift):
    half = near[0].shape[0] // 2
    return send(near[0][:half], shift(1)), send(near[1][half:], shift(-1))


def ring_join(own, near, far, where):
    rows, half = own.shape[0], own.shape[0] // 2
    out = jnp.zeros((4 * rows, own.shape[1]), own.dtype)
    out = lax.dynamic_update_slice(out, own, (rows * where, 0))
    out = lax.dynamic_update_slice(out, near[0], (rows * ((where + 3) % 4), 0))
    out = lax.dynamic_update_slice(out, near[1], (rows * ((where + 1) % 4), 0))
    across = rows * ((where + 2) % 4)
    out = lax.dynamic_update_slice(out, far[0], (across, 0))
    return lax.dynamic_update_slice(out, far[1], (across + half, 0))


def z_ring(k):
    return [(device(a, b, c, 0), device(a, b, (c + k) % 4, 0)) for a, b, c in CHIPS]


def y_ring(k):
    return [(device(a, b, c, d), device(a, (b + k) % 4, c, d)) for a, b, c, d in ALL]


def y_ring_one(k):
    return [(device(a, b, c, 0), device(a, (b + k) % 4, c, 0)) for a, b, c in CHIPS]


def to_other_core(block, core):
    other = send(block, [(device(a, b, c, 0), device(a, b, c, 1)) for a, b, c in CHIPS])
    return jnp.where(core == 0, block, other)


def choose(own, parts, tests):
    for part, test in zip(parts, tests):
        own = jnp.where(test, part, own)
    return own


def ordered(own, other, first):
    return jnp.where(first, jnp.concatenate([own, other], axis=0), jnp.concatenate([other, own], axis=0))


def body(covariance, obs_cells, pred_cells, targets, cross_sum, prior_mean):
    tile_size = covariance.shape[0]
    slab = targets.shape[0]
    width = targets.shape[1]
    row_index = lax.axis_index("row")
    column_index = lax.axis_index("col")
    z, x_lo, core = row_index // 4, (row_index // 2) % 2, row_index % 2
    y, x_hi = column_index // 2, column_index % 2
    x = 2 * x_hi + x_lo

    row_wide = covariance[:, :tile_size]
    quarter = tile_size // 4
    half = tile_size // 2

    packed = jnp.concatenate(
        [
            row_wide[:STRIP],
            jnp.concatenate([row_wide[STRIP:half, STRIP:], row_wide[3 * STRIP :, 3 * STRIP :]], axis=1),
            jnp.concatenate([row_wide[half : half + BLOCK, half:], row_wide[half + BLOCK : 3 * STRIP, half:]], axis=1),
        ],
        axis=0,
    )
    rows = packed.shape[0] // 4
    lead_parts = [send(packed[rows * q : rows * (q + 1)], [(0, device(0, 0, q, 0))]) for q in (1, 3, 2)]

    cells = jnp.pad(obs_cells.astype(jnp.float32).reshape(1, -1), ((0, 7), (0, targets.shape[1] * 2)))
    cells = cells.reshape(8, -1)
    shard = jnp.concatenate([jnp.concatenate([targets, cross_sum], axis=1), cells], axis=0)
    shard_parts = [
        send(shard, [(device(a, b, 0, 0), device(a, b, k, 0)) for a in (0, 2) for b in range(4)]) for k in (1, 3, 2)
    ]
    col_parts = [
        send(
            covariance[quarter * q : quarter * (q + 1)],
            [(device(a, b, 0, 0), device(a, b, q, 0)) for a in (0, 2) for b in range(4)],
        )
        for q in (1, 3, 2)
    ]
    row_parts = [
        send(
            row_wide[quarter * q : quarter * (q + 1)],
            [(device(a, 0, c, d), device(a, q, c, d)) for a in (0, 1) for c in range(4) for d in range(2)],
        )
        for q in (1, 3, 2)
    ]

    order = (1, 3, 2)
    lead = choose(packed[:rows], lead_parts, [z == q for q in order])
    parts = [send(lead, [(device(0, 0, c, 0), device(0, k, c, 0)) for c in range(4)]) for k in order]
    lead = choose(lead, parts, [y == k for k in order])
    lead, shard_parts = tick(lead, shard_parts)
    parts = [
        send(lead, [(device(0, b, c, 0), device(k, b, c, 0)) for b in range(4) for c in range(4)]) for k in order
    ]
    shard = choose(shard, shard_parts, [z == k for k in order])
    part = send(
        shard, [(device(a, b, c, 0), device(a + 1, b, c, 0)) for a in (0, 2) for b in range(4) for c in range(4)]
    )
    shard = jnp.where(x_lo == 0, shard, part)
    lead = choose(lead, parts, [x == k for k in order])
    near = ring_near(lead, z_ring)
    lead, near, shard, col_parts, row_parts = tick(lead, near, shard, col_parts, row_parts)
    far = ring_far(near, z_ring)
    shard = to_other_core(shard, core)
    col_own = choose(covariance[:quarter], col_parts, [z == q for q in order])
    row_own = choose(row_wide[:quarter], row_parts, [y == q for q in order])
    packed = to_other_core(ring_join(lead, near, far, z), core)
    col_cross = send(
        col_own, [(device(a, b, c, 0), device(a + 1, b, c, 0)) for a in (0, 2) for b in range(4) for c in range(4)]
    )
    row_cross = send(
        row_own,
        [(device(a, b, c, d), device(a + 2, b, c, d)) for a in (0, 1) for b in range(4) for c in range(4) for d in range(2)],
    )
    part = send(shard, [(device(a, b, c, d), device(a ^ 2, b, c, d)) for a, b, c, d in ALL])
    shard = ordered(shard, part, x_hi == 0)

    top_half = factor_half(packed)
    top_half, shard, col_cross, row_cross = tick(top_half, shard, col_cross, row_cross)
    col_own = jnp.where(x_lo == 0, col_own, col_cross)
    row_own = jnp.where(x_hi == 0, row_own, row_cross)
    row_near = ring_near(row_own, y_ring)
    col_near = ring_near(col_own, z_ring)
    shard_near = ring_near(shard, y_ring)
    inverse = factor_half(packed, top_half)
    inverse, shard_near, col_near, row_near = tick(inverse, shard_near, col_near, row_near)
    row_far = ring_far(row_near, y_ring)
    col_far = ring_far(col_near, z_ring)
    shard_far = ring_far(shard_near, y_ring)
    col_far, row_far, shard_far = tick(col_far, row_far, shard_far)
    row_tile = ring_join(row_own, row_near, row_far, y)
    column_tile = to_other_core(ring_join(col_own, col_near, col_far, z), core)
    halves = [column_tile[:, :tile_size], column_tile[:, tile_size:]]
    shards = ring_join(shard, shard_near, shard_far, y).reshape(8, slab + 8, -1)
    top = shards[:, :slab].reshape(tile_size, -1)
    lead_cells = shards[:, slab, : 2 * slab].reshape(8, 2, slab).transpose(1, 0, 2).reshape(2, tile_size)
    kernel = matern_tile(lead_cells, pred_cells.astype(jnp.float32))
    stacked = jnp.concatenate([top[:, :width], kernel - top[:, width:]], axis=1)
    both = jnp.dot(inverse, stacked, precision=HIGH)
    panel_rows = lax.dot_general(row_tile, inverse, (((1,), (1,)), ((), ())), precision=HIGH)
    blocks = []
    for offset in range(2):
        panel = jnp.dot(inverse, halves[offset], precision=HIGH)
        local = covariance[:, offset * tile_size : (offset + 1) * tile_size]
        updated = local - jnp.dot(panel_rows, panel, precision=HIGH)
        updated = jnp.where(row_index == 0, jnp.zeros_like(updated), updated)
        if offset == 0:
            updated = jnp.where(column_index == 0, panel_rows, updated)
        blocks.append(updated)
    factor_state = jnp.concatenate(blocks, axis=1)
    solved = both[:, :width]
    lifted = both[:, width:]
    my_rows = lax.dynamic_slice_in_dim(panel_rows, column_index * slab, slab, 0)
    my_both = lax.dynamic_slice_in_dim(both, column_index * slab, slab, 0)
    change = jnp.dot(my_rows, both, precision=HIGH)
    reduced_targets = jnp.where(row_index == 0, my_both[:, :width], targets - change[:, :width])
    cross_next = jnp.where(row_index == 0, my_both[:, width:], cross_sum + change[:, width:])
    predicted = prior_mean + lax.dot_general(
        lifted, solved, (((0,), (0,)), ((), ())), precision=HIGH
    )
    return (factor_state, reduced_targets, cross_next, predicted)


def solution(mesh):
    in_specs = (
        P("row", "col"),
        P(None, AXES),
        P(),
        P(AXES, None),
        P(AXES, None),
        P(),
    )
    out_specs = (P("row", "col"), P(AXES, None), P(AXES, None), P())
    return jax.shard_map(body, mesh=mesh, in_specs=in_specs, out_specs=out_specs, check_vma=False)
```

```python
import math

import jax
import jax.numpy as jnp
from jax import lax
from jax.experimental import pallas as pl
from jax.experimental.pallas import tpu as pltpu
from jax.sharding import PartitionSpec as P

RANGE = 16
BLOCK = 128
BAND = 32
GROUP = 8
STRIP = 256
AXES = ("row", "col")
HIGHEST = lax.Precision.HIGHEST
HIGH = lax.Precision.HIGH


root_three = math.sqrt(3.0)


def matern_tile(first, second):
    delta_x = first[0][:, None] - second[0][None, :]
    delta_y = first[1][:, None] - second[1][None, :]
    scaled = jnp.sqrt(delta_x * delta_x + delta_y * delta_y) * (root_three / RANGE)
    return (1.0 + scaled) * jnp.exp(-scaled)


def iota(shape, dim):
    return lax.broadcasted_iota(jnp.int32, shape, dim)


def dot(a, b):
    return jnp.dot(a, b, precision=HIGHEST, preferred_element_type=jnp.float32)


def dot_t(a, b):
    return lax.dot_general(
        a, b, (((0,), (0,)), ((), ())), precision=HIGHEST, preferred_element_type=jnp.float32
    )


def eliminate(rows, start):
    shape = (GROUP, BLOCK)
    lane, sub = iota(shape, 1), iota(shape, 0)
    count = len(rows)
    for g in range(count):
        base = start + GROUP * g
        cols = {
            (i, t): jnp.broadcast_to(rows[i][:, base + t : base + t + 1], shape)
            for i in range(g, count)
            for t in range(GROUP)
        }
        scale = jnp.ones(shape, jnp.float32)
        scaled = []
        for t in range(GROUP):
            j = base + t
            diag = cols[g, t]
            pivot = jnp.broadcast_to(diag[t : t + 1, :], shape)
            root = lax.rsqrt(pivot)
            root = root * (1.5 - 0.5 * pivot * root * root)
            inverse = root * root
            scale = jnp.where(sub == t, root, scale)
            own = jnp.where((lane == j) & (sub >= t), jnp.where(sub == t, 1.0, 0.0), rows[g])
            row = jnp.broadcast_to(own[t : t + 1, :], shape) * inverse
            below = jnp.where(sub > t, diag, 0.0)
            rows[g] = own - below * row
            scaled.append(jnp.where((lane > j) & (lane < base + GROUP), 0.0, row))
            for u in range(t + 1, GROUP):
                factor = jnp.broadcast_to(diag[u : u + 1, :], shape) * inverse
                for i in range(g, count):
                    cols[i, u] = cols[i, u] - (below if i == g else cols[i, t]) * factor
        for i in range(g + 1, count):
            rest = jnp.where((lane >= base) & (lane < base + GROUP), 0.0, rows[i])
            for t in range(GROUP):
                rest = rest - cols[i, t] * scaled[t]
            rows[i] = rest
        rows[g] = rows[g] * scale
    return rows


def invert_block(block):
    lane, sub = iota((BAND, BLOCK), 1), iota((BAND, BLOCK), 0)
    wide = iota((BLOCK, BLOCK), 1)
    done = []
    for start in range(0, BLOCK, BAND):
        rows = [block[start + g : start + g + GROUP, :] for g in range(0, BAND, GROUP)]
        band = jnp.concatenate(eliminate(rows, start), axis=0)
        upper = jnp.where(lane >= start + BAND, band, 0.0)
        clean = jnp.where((lane < start + BAND) & (lane > start + sub), 0.0, band)
        if start + BAND < BLOCK:
            block = jnp.where((wide >= start) & (wide < start + BAND), 0.0, block) - dot_t(upper, clean)
        done.append(jnp.where(lane > start + sub, 0.0, band))
    return jnp.concatenate(done, axis=0)


def factor_kernel(flag, tile, out, work):
    size = tile.shape[0]
    count = size // BLOCK

    @pl.when(flag[0] == 1)
    def _():
        work[...] = tile[...]
        lane = iota((BLOCK, size), 1)

        def step(k, _):
            here = pl.multiple_of(k * BLOCK, BLOCK)
            inverse = invert_block(work[pl.ds(here, BLOCK), pl.ds(here, BLOCK)])
            work[pl.ds(here, BLOCK), :] = dot(inverse, work[pl.ds(here, BLOCK), :])
            work[pl.ds(here, BLOCK), pl.ds(here, BLOCK)] = inverse

            def update(i, _):
                at = pl.multiple_of(i * BLOCK, BLOCK)
                factor = work[pl.ds(here, BLOCK), pl.ds(at, BLOCK)].T
                rest = work[pl.ds(at, BLOCK), :]
                rest = jnp.where((lane >= here) & (lane < here + BLOCK), 0.0, rest)
                work[pl.ds(at, BLOCK), :] = rest - dot(factor, work[pl.ds(here, BLOCK), :])
                return 0

            lax.fori_loop(k + 1, count, update, 0)
            work[pl.ds(here, BLOCK), :] = jnp.where(lane > here + iota((BLOCK, size), 0), 0.0, work[pl.ds(here, BLOCK), :])
            return 0

        lax.fori_loop(0, count, step, 0)
        half = STRIP // 2
        out[:STRIP, :] = work[3 * STRIP :, :]
        out[STRIP : 2 * STRIP, : 3 * STRIP] = work[2 * STRIP : 3 * STRIP, : 3 * STRIP]
        out[STRIP : 2 * STRIP, 3 * STRIP :] = work[:STRIP, :STRIP]
        out[2 * STRIP :, : 2 * STRIP] = work[STRIP : STRIP + half, : 2 * STRIP]
        out[2 * STRIP :, 2 * STRIP :] = work[STRIP + half : 2 * STRIP, : 2 * STRIP]


def factor_tile(flag, tile):
    size = tile.shape[0]
    return pl.pallas_call(
        factor_kernel,
        grid=(1,),
        out_shape=jax.ShapeDtypeStruct((5 * STRIP // 2, size), jnp.float32),
        in_specs=[
            pl.BlockSpec(memory_space=pltpu.SMEM),
            pl.BlockSpec((size, size), lambda i: (0, 0), pipeline_mode=pl.Buffered(1)),
        ],
        out_specs=pl.BlockSpec((5 * STRIP // 2, size), lambda i: (0, 0), pipeline_mode=pl.Buffered(1)),
        scratch_shapes=[pltpu.VMEM((size, size), jnp.float32)],
        compiler_params=pltpu.CompilerParams(vmem_limit_bytes=40 << 20),
        name="factor_tile",
    )(flag, tile)


def split(value):
    high = value.astype(jnp.bfloat16)
    return high, (value - high.astype(jnp.float32)).astype(jnp.bfloat16)


def product(a, b, dims=((1,), (0,))):
    def one(x, y):
        return lax.dot_general(x, y, (dims, ((), ())), preferred_element_type=jnp.float32)

    return one(a[0], b[0]) + (one(a[0], b[1]) + one(a[1], b[0]))


def update_kernel(place, packed, rows, stacked, near, other, local, out, both, change, w_hi, w_lo, p_hi, p_lo, c_hi, c_lo):
    step = pl.program_id(0)
    size = rows.shape[0]
    slab = change.shape[0]
    bands = [(STRIP * i, STRIP * (i + 1)) for i in range(size // STRIP)]

    def below(lo, hi):
        return w_hi[lo:hi, :hi], w_lo[lo:hi, :hi]

    @pl.when(step == 0)
    def _():
        half = STRIP // 2
        w_hi[3 * STRIP :, :], w_lo[3 * STRIP :, :] = split(packed[:STRIP, :])
        w_hi[2 * STRIP : 3 * STRIP, : 3 * STRIP], w_lo[2 * STRIP : 3 * STRIP, : 3 * STRIP] = split(
            packed[STRIP : 2 * STRIP, : 3 * STRIP]
        )
        w_hi[:STRIP, :STRIP], w_lo[:STRIP, :STRIP] = split(packed[STRIP : 2 * STRIP, 3 * STRIP :])
        for k in range(2):
            at = STRIP + half * k
            w_hi[at : at + half, : 2 * STRIP], w_lo[at : at + half, : 2 * STRIP] = split(
                packed[2 * STRIP :, 2 * STRIP * k : 2 * STRIP * (k + 1)]
            )
        for lo, hi in bands:
            panel = product(split(rows[:, :hi]), below(lo, hi), ((1,), (1,)))
            p_hi[:, lo:hi], p_lo[:, lo:hi] = split(panel)
            both[lo:hi, :] = product(below(lo, hi), split(stacked[:hi, :]))
        mine = pl.ds(pl.multiple_of(place[1] * slab, slab), slab)
        change[...] = product((p_hi[mine, :], p_lo[mine, :]), split(both[...]))

    @pl.when(step > 0)
    def _():
        column = jnp.where(place[2] == 0, near[...], other[...])
        c_hi[...], c_lo[...] = split(column)
        for lo, hi in reversed(bands):
            panel = product(below(lo, hi), (c_hi[:hi, :], c_lo[:hi, :]))
            c_hi[lo:hi, :], c_lo[lo:hi, :] = split(panel)
        left = (place[1] == 0) & (step < 3)

        @pl.when(jnp.logical_not(left) & (place[0] == 0))
        def _():
            out[...] = jnp.zeros_like(out)

        @pl.when(jnp.logical_not(left) & (place[0] != 0))
        def _():
            for lo, hi in bands:
                out[lo:hi, :] = local[lo:hi, :] - product((p_hi[lo:hi, :], p_lo[lo:hi, :]), (c_hi[...], c_lo[...]))

        @pl.when(left & (step == 1))
        def _():
            width = out.shape[1]
            out[...] = p_hi[:, :width].astype(jnp.float32) + p_lo[:, :width].astype(jnp.float32)

        @pl.when(left & (step == 2))
        def _():
            width = out.shape[1]
            out[...] = p_hi[:, width:].astype(jnp.float32) + p_lo[:, width:].astype(jnp.float32)


def update(place, packed, rows, stacked, near, other, local, slab):
    size, wide = local.shape
    block = size // 2
    right = stacked.shape[1]

    def whole(shape):
        return pl.BlockSpec(shape, lambda i: (0, 0), pipeline_mode=pl.Buffered(1))

    columns = pl.BlockSpec((size, block), lambda i: (0, jnp.maximum(i - 1, 0)))
    part = pltpu.VMEM((size, size), jnp.bfloat16)
    thin = pltpu.VMEM((size, block), jnp.bfloat16)
    return pl.pallas_call(
        update_kernel,
        grid=(1 + wide // block,),
        in_specs=[
            pl.BlockSpec(memory_space=pltpu.SMEM),
            whole(packed.shape),
            whole(rows.shape),
            whole(stacked.shape),
            columns,
            columns,
            columns,
        ],
        out_specs=[
            columns,
            pl.BlockSpec((size, right), lambda i: (0, 0)),
            pl.BlockSpec((slab, right), lambda i: (0, 0)),
        ],
        out_shape=[
            jax.ShapeDtypeStruct((size, wide), jnp.float32),
            jax.ShapeDtypeStruct((size, right), jnp.float32),
            jax.ShapeDtypeStruct((slab, right), jnp.float32),
        ],
        scratch_shapes=[part, part, part, part, thin, thin],
        compiler_params=pltpu.CompilerParams(vmem_limit_bytes=58 << 20, dimension_semantics=("arbitrary",)),
        name="update",
    )(place, packed, rows, stacked, near, other, local)


def device(x, y, z, core):
    return (z * 4 + (x % 2) * 2 + core) * 8 + y * 2 + x // 2


def send(block, pairs):
    return lax.ppermute(block, AXES, pairs)


def pick(options, index):
    out = options[0]
    for k in range(1, len(options)):
        out = jnp.where(index == k, options[k], out)
    return out


CHIPS = [(x, y, z) for x in range(4) for y in range(4) for z in range(4)]
ALL = [(x, y, z, k) for x, y, z in CHIPS for k in range(2)]


def tick(*groups):
    return lax.optimization_barrier(groups)


def ring_near(own, shift):
    return send(own, shift(1)), send(own, shift(-1))


def ring_far(near, shift):
    half = near[0].shape[0] // 2
    return send(near[0][:half], shift(1)), send(near[1][half:], shift(-1))


def ring_join(own, near, far, where):
    rows, half = own.shape[0], own.shape[0] // 2
    out = jnp.zeros((4 * rows, own.shape[1]), own.dtype)
    out = lax.dynamic_update_slice(out, own, (rows * where, 0))
    out = lax.dynamic_update_slice(out, near[0], (rows * ((where + 3) % 4), 0))
    out = lax.dynamic_update_slice(out, near[1], (rows * ((where + 1) % 4), 0))
    across = rows * ((where + 2) % 4)
    out = lax.dynamic_update_slice(out, far[0], (across, 0))
    return lax.dynamic_update_slice(out, far[1], (across + half, 0))


def z_ring(k):
    return [(device(a, b, c, 0), device(a, b, (c + k) % 4, 0)) for a, b, c in CHIPS]


def y_ring(k):
    return [(device(a, b, c, d), device(a, (b + k) % 4, c, d)) for a, b, c, d in ALL]


def y_ring_one(k):
    return [(device(a, b, c, 0), device(a, (b + k) % 4, c, 0)) for a, b, c in CHIPS]


def to_other_core(block, core):
    other = send(block, [(device(a, b, c, 0), device(a, b, c, 1)) for a, b, c in CHIPS])
    return jnp.where(core == 0, block, other)


def choose(own, parts, tests):
    for part, test in zip(parts, tests):
        own = jnp.where(test, part, own)
    return own


def ordered(own, other, first):
    return jnp.where(first, jnp.concatenate([own, other], axis=0), jnp.concatenate([other, own], axis=0))


def body(covariance, obs_cells, pred_cells, targets, cross_sum, prior_mean):
    tile_size = covariance.shape[0]
    slab = targets.shape[0]
    width = targets.shape[1]
    row_index = lax.axis_index("row")
    column_index = lax.axis_index("col")
    z, x_lo, core = row_index // 4, (row_index // 2) % 2, row_index % 2
    y, x_hi = column_index // 2, column_index % 2
    x = 2 * x_hi + x_lo

    row_wide = covariance[:, :tile_size]
    quarter = tile_size // 4
    order = (1, 3, 2)
    crossing = [(device(a, b, c, 0), device(a + 1, b, c, 0)) for a in (0, 2) for b in range(4) for c in range(4)]
    first = (row_index == 0) & (column_index == 0)
    others = [(a, b, c, d) for a, b, c, d in ALL if (a % 2, c, d) != (0, 0, 0)]

    def y_ring_others(k):
        return [(device(a, b, c, d), device(a, (b + k) % 4, c, d)) for a, b, c, d in others]

    col_parts = [
        send(
            covariance[quarter * q : quarter * (q + 1)],
            [(device(a, b, 0, 0), device(a, b, q, 0)) for a in (0, 2) for b in range(4)],
        )
        for q in order
    ]
    cells = jnp.pad(obs_cells.astype(jnp.float32).reshape(1, -1), ((0, 7), (0, 2 * width)))
    shard = jnp.concatenate([jnp.concatenate([targets, cross_sum], axis=1), cells], axis=0)
    shard_parts = [
        send(shard, [(device(a, b, 0, 0), device(a, b, k, 0)) for a in (0, 2) for b in range(4)]) for k in order
    ]
    packed = factor_tile(first.astype(jnp.int32).reshape(1), covariance)

    slices = [row_wide[quarter * q : quarter * (q + 1)] for q in order]
    packed, slices = tick(packed, slices)
    row_parts = [
        send(part, [(device(a, 0, c, d), device(a, q, c, d)) for a, b, c, d in others if b == 0 and a < 2])
        for part, q in zip(slices, order)
    ]
    rows = packed.shape[0] // 4
    parts = [send(packed[rows * q : rows * (q + 1)], [(0, device(0, 0, q, 0))]) for q in order]
    lead = choose(packed[:rows], parts, [z == q for q in order])
    lead, col_parts, shard_parts = tick(lead, col_parts, shard_parts)

    parts = [send(lead, [(device(0, 0, c, 0), device(0, k, c, 0)) for c in range(4)]) for k in order]
    lead = choose(lead, parts, [y == k for k in order])
    col_own = choose(covariance[:quarter], col_parts, [z == q for q in order])
    col_cross = send(col_own, crossing)
    shard = choose(shard, shard_parts, [z == k for k in order])
    part = send(shard, crossing)
    shard = jnp.where(x_lo == 0, shard, part)
    row_own = choose(row_wide[:quarter], row_parts, [y == q for q in order])
    row_cross = send(row_own, [(device(a, b, c, d), device(a + 2, b, c, d)) for a, b, c, d in others if a < 2])
    lead, shard = tick(lead, shard)
    parts = [
        send(lead, [(device(0, b, c, 0), device(k, b, c, 0)) for b in range(4) for c in range(4)]) for k in order
    ]
    lead = choose(lead, parts, [x == k for k in order])
    shard = to_other_core(shard, core)
    lead, shard, col_cross, row_cross = tick(lead, shard, col_cross, row_cross)

    lead_near = ring_near(lead, z_ring)
    part = send(shard, [(device(a, b, c, d), device(a ^ 2, b, c, d)) for a, b, c, d in ALL])
    col_own = jnp.where(x_lo == 0, col_own, col_cross)
    col_near = ring_near(col_own, z_ring)
    row_own = jnp.where(x_hi == 0, row_own, row_cross)
    row_near = ring_near(row_own, y_ring_others)
    lead_near, part = tick(lead_near, part)
    lead_far = ring_far(lead_near, z_ring)
    shard = ordered(shard, part, x_hi == 0)
    shard_near = ring_near(shard, y_ring)
    lead_far, col_near, row_near, shard_near = tick(lead_far, col_near, row_near, shard_near)
    col_far = ring_far(col_near, z_ring)
    row_far = ring_far(row_near, y_ring_others)
    shard_far = ring_far(shard_near, y_ring)
    packed = to_other_core(ring_join(lead, lead_near, lead_far, z), core)
    packed, col_far, row_far, shard_far = tick(packed, col_far, row_far, shard_far)
    column_near = ring_join(col_own, col_near, col_far, z)
    column_other = send(column_near, [(device(a, b, c, 0), device(a, b, c, 1)) for a, b, c in CHIPS])
    row_tile = jnp.where(first, row_wide, ring_join(row_own, row_near, row_far, y))
    shards = ring_join(shard, shard_near, shard_far, y).reshape(8, slab + 8, -1)
    top = shards[:, :slab].reshape(tile_size, -1)
    lead_cells = shards[:, slab, : 2 * slab].reshape(8, 2, slab).transpose(1, 0, 2).reshape(2, tile_size)

    kernel = matern_tile(lead_cells, pred_cells.astype(jnp.float32))
    stacked = jnp.concatenate([top[:, :width], kernel - top[:, width:]], axis=1)
    place = jnp.stack([row_index, column_index, core]).astype(jnp.int32)
    factor_state, both, change = update(
        place, packed, row_tile, stacked, column_near, column_other, covariance, slab
    )
    solved = both[:, :width]
    lifted = both[:, width:]
    my_both = lax.dynamic_slice_in_dim(both, column_index * slab, slab, 0)
    reduced_targets = jnp.where(row_index == 0, my_both[:, :width], targets - change[:, :width])
    cross_next = jnp.where(row_index == 0, my_both[:, width:], cross_sum + change[:, width:])
    predicted = prior_mean + lax.dot_general(
        lifted, solved, (((0,), (0,)), ((), ())), precision=HIGH
    )
    return (factor_state, reduced_targets, cross_next, predicted)


def solution(mesh):
    in_specs = (
        P("row", "col"),
        P(None, AXES),
        P(),
        P(AXES, None),
        P(AXES, None),
        P(),
    )
    out_specs = (P("row", "col"), P(AXES, None), P(AXES, None), P())
    return jax.shard_map(body, mesh=mesh, in_specs=in_specs, out_specs=out_specs, check_vma=False)
```

```python
import math

import jax
import jax.numpy as jnp
from jax import lax
from jax.experimental import pallas as pl
from jax.experimental.pallas import tpu as pltpu
from jax.sharding import PartitionSpec as P

RANGE = 16
BLOCK = 128
BAND = 32
GROUP = 8
STRIP = 256
AXES = ("row", "col")
HIGHEST = lax.Precision.HIGHEST
HIGH = lax.Precision.HIGH


root_three = math.sqrt(3.0)


def matern_tile(first, second):
    delta_x = first[0][:, None] - second[0][None, :]
    delta_y = first[1][:, None] - second[1][None, :]
    scaled = jnp.sqrt(delta_x * delta_x + delta_y * delta_y) * (root_three / RANGE)
    return (1.0 + scaled) * jnp.exp(-scaled)


def iota(shape, dim):
    return lax.broadcasted_iota(jnp.int32, shape, dim)


def dot(a, b):
    return jnp.dot(a, b, precision=HIGHEST, preferred_element_type=jnp.float32)


def dot_t(a, b):
    return lax.dot_general(
        a, b, (((0,), (0,)), ((), ())), precision=HIGHEST, preferred_element_type=jnp.float32
    )


def eliminate(rows, start):
    shape = (GROUP, BLOCK)
    lane, sub = iota(shape, 1), iota(shape, 0)
    count = len(rows)
    for g in range(count):
        base = start + GROUP * g
        cols = {
            (i, t): jnp.broadcast_to(rows[i][:, base + t : base + t + 1], shape)
            for i in range(g, count)
            for t in range(GROUP)
        }
        scale = jnp.ones(shape, jnp.float32)
        scaled = []
        for t in range(GROUP):
            j = base + t
            diag = cols[g, t]
            pivot = jnp.broadcast_to(diag[t : t + 1, :], shape)
            root = lax.rsqrt(pivot)
            root = root * (1.5 - 0.5 * pivot * root * root)
            inverse = root * root
            scale = jnp.where(sub == t, root, scale)
            own = jnp.where((lane == j) & (sub >= t), jnp.where(sub == t, 1.0, 0.0), rows[g])
            row = jnp.broadcast_to(own[t : t + 1, :], shape) * inverse
            below = jnp.where(sub > t, diag, 0.0)
            rows[g] = own - below * row
            scaled.append(jnp.where((lane > j) & (lane < base + GROUP), 0.0, row))
            for u in range(t + 1, GROUP):
                factor = jnp.broadcast_to(diag[u : u + 1, :], shape) * inverse
                for i in range(g, count):
                    cols[i, u] = cols[i, u] - (below if i == g else cols[i, t]) * factor
        for i in range(g + 1, count):
            rest = jnp.where((lane >= base) & (lane < base + GROUP), 0.0, rows[i])
            for t in range(GROUP):
                rest = rest - cols[i, t] * scaled[t]
            rows[i] = rest
        rows[g] = rows[g] * scale
    return rows


def invert_block(block):
    lane, sub = iota((BAND, BLOCK), 1), iota((BAND, BLOCK), 0)
    wide = iota((BLOCK, BLOCK), 1)
    done = []
    for start in range(0, BLOCK, BAND):
        rows = [block[start + g : start + g + GROUP, :] for g in range(0, BAND, GROUP)]
        band = jnp.concatenate(eliminate(rows, start), axis=0)
        upper = jnp.where(lane >= start + BAND, band, 0.0)
        clean = jnp.where((lane < start + BAND) & (lane > start + sub), 0.0, band)
        if start + BAND < BLOCK:
            block = jnp.where((wide >= start) & (wide < start + BAND), 0.0, block) - dot_t(upper, clean)
        done.append(jnp.where(lane > start + sub, 0.0, band))
    return jnp.concatenate(done, axis=0)


def factor_kernel(flag, tile, out, work):
    size = tile.shape[0]
    count = size // BLOCK

    @pl.when(flag[0] == 1)
    def _():
        work[...] = tile[...]
        lane = iota((BLOCK, size), 1)

        def step(k, _):
            here = pl.multiple_of(k * BLOCK, BLOCK)
            inverse = invert_block(work[pl.ds(here, BLOCK), pl.ds(here, BLOCK)])
            work[pl.ds(here, BLOCK), :] = dot(inverse, work[pl.ds(here, BLOCK), :])
            work[pl.ds(here, BLOCK), pl.ds(here, BLOCK)] = inverse

            def update(i, _):
                at = pl.multiple_of(i * BLOCK, BLOCK)
                factor = work[pl.ds(here, BLOCK), pl.ds(at, BLOCK)].T
                rest = work[pl.ds(at, BLOCK), :]
                rest = jnp.where((lane >= here) & (lane < here + BLOCK), 0.0, rest)
                work[pl.ds(at, BLOCK), :] = rest - dot(factor, work[pl.ds(here, BLOCK), :])
                return 0

            lax.fori_loop(k + 1, count, update, 0)
            work[pl.ds(here, BLOCK), :] = jnp.where(lane > here + iota((BLOCK, size), 0), 0.0, work[pl.ds(here, BLOCK), :])
            return 0

        lax.fori_loop(0, count, step, 0)
        half = STRIP // 2
        out[:STRIP, :] = work[3 * STRIP :, :]
        out[STRIP : 2 * STRIP, : 3 * STRIP] = work[2 * STRIP : 3 * STRIP, : 3 * STRIP]
        out[STRIP : 2 * STRIP, 3 * STRIP :] = work[:STRIP, :STRIP]
        out[2 * STRIP :, : 2 * STRIP] = work[STRIP : STRIP + half, : 2 * STRIP]
        out[2 * STRIP :, 2 * STRIP :] = work[STRIP + half : 2 * STRIP, : 2 * STRIP]


def factor_tile(flag, tile):
    size = tile.shape[0]
    return pl.pallas_call(
        factor_kernel,
        grid=(1,),
        out_shape=jax.ShapeDtypeStruct((5 * STRIP // 2, size), jnp.float32),
        in_specs=[
            pl.BlockSpec(memory_space=pltpu.SMEM),
            pl.BlockSpec((size, size), lambda i: (0, 0), pipeline_mode=pl.Buffered(1)),
        ],
        out_specs=pl.BlockSpec((5 * STRIP // 2, size), lambda i: (0, 0), pipeline_mode=pl.Buffered(1)),
        scratch_shapes=[pltpu.VMEM((size, size), jnp.float32)],
        compiler_params=pltpu.CompilerParams(vmem_limit_bytes=40 << 20),
        name="factor_tile",
    )(flag, tile)


def split(value):
    high = value.astype(jnp.bfloat16)
    return high, (value - high.astype(jnp.float32)).astype(jnp.bfloat16)


def product(a, b, dims=((1,), (0,))):
    def one(x, y):
        return lax.dot_general(x, y, (dims, ((), ())), preferred_element_type=jnp.float32)

    return one(a[0], b[0]) + (one(a[0], b[1]) + one(a[1], b[0]))


def update_kernel(place, packed, rows, stacked, near, other, local, out, both, change, w_hi, w_lo, p_hi, p_lo, c_hi, c_lo):
    step = pl.program_id(0)
    size = rows.shape[0]
    slab = change.shape[0]
    bands = [(STRIP * i, STRIP * (i + 1)) for i in range(size // STRIP)]

    def below(lo, hi):
        return w_hi[lo:hi, :hi], w_lo[lo:hi, :hi]

    @pl.when(step == 0)
    def _():
        half = STRIP // 2
        w_hi[3 * STRIP :, :], w_lo[3 * STRIP :, :] = split(packed[:STRIP, :])
        w_hi[2 * STRIP : 3 * STRIP, : 3 * STRIP], w_lo[2 * STRIP : 3 * STRIP, : 3 * STRIP] = split(
            packed[STRIP : 2 * STRIP, : 3 * STRIP]
        )
        w_hi[:STRIP, :STRIP], w_lo[:STRIP, :STRIP] = split(packed[STRIP : 2 * STRIP, 3 * STRIP :])
        for k in range(2):
            at = STRIP + half * k
            w_hi[at : at + half, : 2 * STRIP], w_lo[at : at + half, : 2 * STRIP] = split(
                packed[2 * STRIP :, 2 * STRIP * k : 2 * STRIP * (k + 1)]
            )
        for lo, hi in bands:
            panel = product(split(rows[:, :hi]), below(lo, hi), ((1,), (1,)))
            p_hi[:, lo:hi], p_lo[:, lo:hi] = split(panel)
            both[lo:hi, :] = product(below(lo, hi), split(stacked[:hi, :]))
        mine = pl.ds(pl.multiple_of(place[1] * slab, slab), slab)
        change[...] = product((p_hi[mine, :], p_lo[mine, :]), split(both[...]))

    @pl.when(step > 0)
    def _():
        column = jnp.where(place[2] == 0, near[...], other[...])
        c_hi[...], c_lo[...] = split(column)
        for lo, hi in reversed(bands):
            panel = product(below(lo, hi), (c_hi[:hi, :], c_lo[:hi, :]))
            c_hi[lo:hi, :], c_lo[lo:hi, :] = split(panel)
        left = (place[1] == 0) & (step < 3)

        @pl.when(jnp.logical_not(left) & (place[0] == 0))
        def _():
            out[...] = jnp.zeros_like(out)

        @pl.when(jnp.logical_not(left) & (place[0] != 0))
        def _():
            for lo, hi in bands:
                out[lo:hi, :] = local[lo:hi, :] - product((p_hi[lo:hi, :], p_lo[lo:hi, :]), (c_hi[...], c_lo[...]))

        @pl.when(left & (step == 1))
        def _():
            width = out.shape[1]
            out[...] = p_hi[:, :width].astype(jnp.float32) + p_lo[:, :width].astype(jnp.float32)

        @pl.when(left & (step == 2))
        def _():
            width = out.shape[1]
            out[...] = p_hi[:, width:].astype(jnp.float32) + p_lo[:, width:].astype(jnp.float32)


def update(place, packed, rows, stacked, near, other, local, slab):
    size, wide = local.shape
    block = size // 2
    right = stacked.shape[1]

    def whole(shape):
        return pl.BlockSpec(shape, lambda i: (0, 0), pipeline_mode=pl.Buffered(1))

    columns = pl.BlockSpec((size, block), lambda i: (0, jnp.maximum(i - 1, 0)))
    part = pltpu.VMEM((size, size), jnp.bfloat16)
    thin = pltpu.VMEM((size, block), jnp.bfloat16)
    return pl.pallas_call(
        update_kernel,
        grid=(1 + wide // block,),
        in_specs=[
            pl.BlockSpec(memory_space=pltpu.SMEM),
            whole(packed.shape),
            whole(rows.shape),
            whole(stacked.shape),
            columns,
            columns,
            columns,
        ],
        out_specs=[
            columns,
            pl.BlockSpec((size, right), lambda i: (0, 0)),
            pl.BlockSpec((slab, right), lambda i: (0, 0)),
        ],
        out_shape=[
            jax.ShapeDtypeStruct((size, wide), jnp.float32),
            jax.ShapeDtypeStruct((size, right), jnp.float32),
            jax.ShapeDtypeStruct((slab, right), jnp.float32),
        ],
        scratch_shapes=[part, part, part, part, thin, thin],
        compiler_params=pltpu.CompilerParams(vmem_limit_bytes=58 << 20, dimension_semantics=("arbitrary",)),
        name="update",
    )(place, packed, rows, stacked, near, other, local)


def device(x, y, z, core):
    return (z * 4 + (x % 2) * 2 + core) * 8 + y * 2 + x // 2


def send(block, pairs):
    return lax.ppermute(block, AXES, pairs)


def pick(options, index):
    out = options[0]
    for k in range(1, len(options)):
        out = jnp.where(index == k, options[k], out)
    return out


CHIPS = [(x, y, z) for x in range(4) for y in range(4) for z in range(4)]
ALL = [(x, y, z, k) for x, y, z in CHIPS for k in range(2)]


def tick(*groups):
    return lax.optimization_barrier(groups)


def ring_near(own, shift):
    return send(own, shift(1)), send(own, shift(-1))


def ring_far(near, shift):
    half = near[0].shape[0] // 2
    return send(near[0][:half], shift(1)), send(near[1][half:], shift(-1))


def ring_join(own, near, far, where):
    rows, half = own.shape[0], own.shape[0] // 2
    out = jnp.zeros((4 * rows, own.shape[1]), own.dtype)
    out = lax.dynamic_update_slice(out, own, (rows * where, 0))
    out = lax.dynamic_update_slice(out, near[0], (rows * ((where + 3) % 4), 0))
    out = lax.dynamic_update_slice(out, near[1], (rows * ((where + 1) % 4), 0))
    across = rows * ((where + 2) % 4)
    out = lax.dynamic_update_slice(out, far[0], (across, 0))
    return lax.dynamic_update_slice(out, far[1], (across + half, 0))


def z_ring(k):
    return [(device(a, b, c, 0), device(a, b, (c + k) % 4, 0)) for a, b, c in CHIPS]


def y_ring(k):
    return [(device(a, b, c, d), device(a, (b + k) % 4, c, d)) for a, b, c, d in ALL]


def y_ring_one(k):
    return [(device(a, b, c, 0), device(a, (b + k) % 4, c, 0)) for a, b, c in CHIPS]


def to_other_core(block, core):
    other = send(block, [(device(a, b, c, 0), device(a, b, c, 1)) for a, b, c in CHIPS])
    return jnp.where(core == 0, block, other)


def choose(own, parts, tests):
    for part, test in zip(parts, tests):
        own = jnp.where(test, part, own)
    return own


def ordered(own, other, first):
    return jnp.where(first, jnp.concatenate([own, other], axis=0), jnp.concatenate([other, own], axis=0))


def body(covariance, obs_cells, pred_cells, targets, cross_sum, prior_mean):
    tile_size = covariance.shape[0]
    slab = targets.shape[0]
    width = targets.shape[1]
    row_index = lax.axis_index("row")
    column_index = lax.axis_index("col")
    z, x_lo, core = row_index // 4, (row_index // 2) % 2, row_index % 2
    y, x_hi = column_index // 2, column_index % 2
    x = 2 * x_hi + x_lo

    row_wide = covariance[:, :tile_size]
    quarter = tile_size // 4
    order = (1, 3, 2)
    crossing = [(device(a, b, c, 0), device(a + 1, b, c, 0)) for a in (0, 2) for b in range(4) for c in range(4)]
    first = (row_index == 0) & (column_index == 0)
    others = [(a, b, c, d) for a, b, c, d in ALL if (a % 2, c, d) != (0, 0, 0)]

    def y_ring_others(k):
        return [(device(a, b, c, d), device(a, (b + k) % 4, c, d)) for a, b, c, d in others]

    col_parts = [
        send(
            covariance[quarter * q : quarter * (q + 1)],
            [(device(a, b, 0, 0), device(a, b, q, 0)) for a in (0, 2) for b in range(4)],
        )
        for q in order
    ]
    cells = jnp.pad(obs_cells.astype(jnp.float32).reshape(1, -1), ((0, 7), (0, 2 * width)))
    shard = jnp.concatenate([jnp.concatenate([targets, cross_sum], axis=1), cells], axis=0)
    packed = factor_tile(first.astype(jnp.int32).reshape(1), covariance)

    slices = [row_wide[quarter * q : quarter * (q + 1)] for q in order]
    packed, slices = tick(packed, slices)
    row_parts = [
        send(part, [(device(a, 0, c, d), device(a, q, c, d)) for a, b, c, d in others if b == 0 and a < 2])
        for part, q in zip(slices, order)
    ]
    packed, row_parts, col_parts, shard = tick(packed, row_parts, col_parts, shard)

    rows = packed.shape[0] // 4
    parts = [send(packed[rows * q : rows * (q + 1)], [(0, device(0, 0, q, 0))]) for q in order]
    col_own = choose(covariance[:quarter], col_parts, [z == q for q in order])
    col_cross = send(col_own, crossing)
    row_own = choose(row_wide[:quarter], row_parts, [y == q for q in order])
    row_cross = send(row_own, [(device(a, b, c, d), device(a + 2, b, c, d)) for a, b, c, d in others if a < 2])
    shard_parts = [
        send(shard, [(device(a, b, 0, 0), device(a, b, k, 0)) for a in (0, 2) for b in range(4)]) for k in order
    ]
    lead = choose(packed[:rows], parts, [z == q for q in order])
    lead, col_cross, shard_parts = tick(lead, col_cross, shard_parts)

    parts = [send(lead, [(device(0, 0, c, 0), device(0, k, c, 0)) for c in range(4)]) for k in order]
    col_own = jnp.where(x_lo == 0, col_own, col_cross)
    col_near = ring_near(col_own, z_ring)
    shard = choose(shard, shard_parts, [z == k for k in order])
    shard_part = send(shard, crossing)
    lead = choose(lead, parts, [y == k for k in order])
    lead, row_cross, shard_part = tick(lead, row_cross, shard_part)

    parts = [
        send(lead, [(device(0, b, c, 0), device(k, b, c, 0)) for b in range(4) for c in range(4)]) for k in order
    ]
    row_own = jnp.where(x_hi == 0, row_own, row_cross)
    row_near = ring_near(row_own, y_ring_others)
    shard = jnp.where(x_lo == 0, shard, shard_part)
    shard_part = send(shard, [(device(a, b, c, 0), device(a, b, c, 1)) for a, b, c in CHIPS])
    lead = choose(lead, parts, [x == k for k in order])
    lead, col_near, shard_part = tick(lead, col_near, shard_part)

    lead_near = ring_near(lead, z_ring)
    col_far = ring_far(col_near, z_ring)
    shard = jnp.where(core == 0, shard, shard_part)
    shard_part = send(shard, [(device(a, b, c, d), device(a ^ 2, b, c, d)) for a, b, c, d in ALL])
    lead_near, row_near, shard_part = tick(lead_near, row_near, shard_part)
    lead_far = ring_far(lead_near, z_ring)
    row_far = ring_far(row_near, y_ring_others)
    shard = ordered(shard, shard_part, x_hi == 0)
    shard_near = ring_near(shard, y_ring)
    lead_far, col_far = tick(lead_far, col_far)
    packed = to_other_core(ring_join(lead, lead_near, lead_far, z), core)
    column_near = ring_join(col_own, col_near, col_far, z)
    column_other = send(column_near, [(device(a, b, c, 0), device(a, b, c, 1)) for a, b, c in CHIPS])
    packed, row_far, shard_near = tick(packed, row_far, shard_near)
    shard_far = ring_far(shard_near, y_ring)
    row_tile = jnp.where(first, row_wide, ring_join(row_own, row_near, row_far, y))
    shards = ring_join(shard, shard_near, shard_far, y).reshape(8, slab + 8, -1)
    top = shards[:, :slab].reshape(tile_size, -1)
    lead_cells = shards[:, slab, : 2 * slab].reshape(8, 2, slab).transpose(1, 0, 2).reshape(2, tile_size)

    kernel = matern_tile(lead_cells, pred_cells.astype(jnp.float32))
    stacked = jnp.concatenate([top[:, :width], kernel - top[:, width:]], axis=1)
    place = jnp.stack([row_index, column_index, core]).astype(jnp.int32)
    factor_state, both, change = update(
        place, packed, row_tile, stacked, column_near, column_other, covariance, slab
    )
    solved = both[:, :width]
    lifted = both[:, width:]
    my_both = lax.dynamic_slice_in_dim(both, column_index * slab, slab, 0)
    reduced_targets = jnp.where(row_index == 0, my_both[:, :width], targets - change[:, :width])
    cross_next = jnp.where(row_index == 0, my_both[:, width:], cross_sum + change[:, width:])
    predicted = prior_mean + lax.dot_general(
        lifted, solved, (((0,), (0,)), ((), ())), precision=HIGH
    )
    return (factor_state, reduced_targets, cross_next, predicted)


def solution(mesh):
    in_specs = (
        P("row", "col"),
        P(None, AXES),
        P(),
        P(AXES, None),
        P(AXES, None),
        P(),
    )
    out_specs = (P("row", "col"), P(AXES, None), P(AXES, None), P())
    return jax.shard_map(body, mesh=mesh, in_specs=in_specs, out_specs=out_specs, check_vma=False)
```
